32 devices in a mesh: member: 2 (over y), tile: 4 (over z), sub: 4 (over x, core).
Axes of the slice: x: 2, y: 2, z: 4, core: 2. Of those that a mesh axis runs over, the one named last changes fastest.
Arguments:
- obs_forcing: bfloat16 [8, 4, 72, 8192], P('member', None, 'sub', 'tile'), parts along dimension 0, may hold values from -6 to 6
- transport_weights: bfloat16 [128, 64, 384], P('tile'), may hold values from -0.25 to 0.25
- block_offsets: int32 [128, 6], P('tile'), may hold values from -4 to 4
- edge_source: int32 [4, 4, 1], replicated, may hold values from 0 to 1
- edge_target: int32 [4, 4, 1], P('tile'), may hold values from 0 to 32, as said below
- edge_rotation: int32 [4, 4, 1], P('tile'), may hold values from 0 to 3
- edge_weight: float32 [4, 4, 1, 64], P('tile'), may hold values from -0.2 to 0.2
- mixing_rate: float32 [72, 8192], P('sub', 'tile'), may hold values from 0.02 to 0.3
- flux_profile: float32 [72], P('sub'), may hold values from 0.01 to 0.1
Outputs:
- adjoint_state: float32 [8, 72, 8192], P('member', 'sub', 'tile'), parts along dimension 0
- flux_grad: float32 [8, 8192], P('member', ('tile', 'sub')), parts along dimension 0
The draws below stay inside these ranges and needn't reach their ends.
There are 2 independent parts, one for each index of `member`. The reference program is written for one: setup_inputs(seed, part) draws one part's arguments, and reference() takes and returns one part's arrays. A program takes and returns all parts, laid end to end along the dimension named above; an argument that names none is the same for every part. Nothing has to cross between parts.
Inputs may be any that keep to these rules, and one draw needn't show every extreme that they name: `edge_target`: 32 marks an empty slot; every other value is below 2. Receiver j has live slots only from the 3 or 4 tiles that border it across cube edges: j + 1 and j - 1 modulo 4, j + 4 // 2 modulo 4, and on some receivers j + 4 // 4 modulo 4; all other slots are empty.
All inputs are finite; a program needn't handle non-finite values.
Results may differ from the reference program's by a relative error of at most 0.015.
Values may be sent and summed in bfloat16 or wider, within the bound.
No kernel may reach another device: no remote copies, remote signals or barrier semaphores. Data moves between devices by JAX's collectives and lax.ppermute only.
A program may use at most 64 MiB of HBM per device.

```python
import math
import jax
import jax.numpy as jnp
from jax import lax

TR = 4
LEV = 72
BLOCK = 64
K = 6
HB = 4
EB = 2
C = 1
STEPS = 16
NOBS = 4
BLK_DEV = 32
TILES = 4
COLS = 8192


def draw_edge_target(key, part):
    base_key = jax.random.fold_in(key, 7)
    extra_key, index_key = jax.random.split(base_key)
    shape_all = (TILES, TILES, C)
    receiver = jnp.arange(TILES, dtype=jnp.int32)[:, None, None]
    sender = jnp.arange(TILES, dtype=jnp.int32)[None, :, None]
    offset = (sender - receiver) % TILES
    extra_flag = jax.random.randint(extra_key, (TILES, 1, 1), 0, 2)
    live_slot = (offset == 1) | (offset == TILES - 1) | (offset == TILES // 2) | (offset == TILES // 4) & (extra_flag == 1)
    local_block = jax.random.randint(index_key, shape_all, 0, EB)
    return jnp.where(live_slot, local_block, BLK_DEV).astype(jnp.int32)


def place_ends(values, own_key, smallest, largest):
    longest = values.shape.index(max(values.shape))
    spots = []
    for shift in (0, 1):
        where = [jax.random.randint(jax.random.fold_in(own_key, axis), (), 0, length) for axis, length in enumerate(values.shape)]
        where[longest] = (where[longest] + shift) % values.shape[longest]
        spots.append(tuple(where))
    return values.at[spots[0]].set(smallest).at[spots[1]].set(largest)


def level_of(key, dims, pieces, least, top_value):
    def one(axis_at, shards_of):
        steps = jax.random.uniform(jax.random.fold_in(jax.random.fold_in(key, 6), axis_at), (shards_of,), jnp.float32, least / len(pieces), top_value / len(pieces))
        return jnp.repeat(jnp.exp(steps), dims[axis_at] // shards_of).reshape((-1,) + (1,) * (len(dims) - axis_at - 1))

    loudness = one(*pieces[0])
    for cut in pieces[1:]:
        loudness = loudness * one(*cut)
    return loudness


def normal_values(stream_key, extent, deviation, limit, shards=(), kind=jnp.bfloat16):
    gain = level_of(stream_key, extent, shards, -0.22, 0.18) if shards else 1.0
    drawn = jax.random.normal(stream_key, extent, jnp.float32) * deviation * gain
    return jnp.minimum(jnp.maximum(drawn, -limit), limit).astype(kind)


def setup_inputs(seed: int = 0, part: int = 0) -> dict:
    seeds = jax.random.split(jax.random.key(seed), 10)
    own_keys = jax.random.split(jax.random.fold_in(seeds[9], part), 10)
    return {
        "obs_forcing": normal_values(own_keys[0], (NOBS, TR, LEV, COLS), 1.0, 6.0, ((2, 4), (3, 4))),
        "transport_weights": normal_values(seeds[1], (TILES * BLK_DEV, BLOCK, K * BLOCK), (7 * BLOCK) ** -0.5, 0.25, ((0, 4),)),
        "block_offsets": place_ends(jax.random.randint(seeds[2], (TILES * BLK_DEV, K), 0 - HB, HB + 1), jax.random.fold_in(seeds[2], 1), 0 - HB, HB).astype(jnp.int32),
        "edge_source": place_ends(jax.random.randint(seeds[3], (TILES, TILES, C), 0, EB), jax.random.fold_in(seeds[3], 1), 0, EB - 1).astype(jnp.int32),
        "edge_target": draw_edge_target(jax.random.fold_in(seeds[9], 71), part),
        "edge_rotation": place_ends(jax.random.randint(seeds[5], (TILES, TILES, C), 0, 4), jax.random.fold_in(seeds[5], 1), 0, 3).astype(jnp.int32),
        "edge_weight": jnp.clip(jax.random.uniform(seeds[6], (TILES, TILES, C, BLOCK), jnp.float32, -0.2, 0.2) * level_of(seeds[6], (TILES, TILES, C, BLOCK), ((0, 4),), -0.4, 0.0), -0.2, 0.2),
        "mixing_rate": jnp.clip(0.02 + 0.28 * jax.random.uniform(seeds[7], (LEV, COLS), jnp.float32) ** level_of(seeds[7], (LEV, COLS), ((0, 4), (1, 4)), -0.2, 0.2), 0.02, 0.3),
        "flux_profile": jnp.clip(jnp.exp(math.log(0.1) - 2.3025851 * jax.random.uniform(seeds[8], (LEV,), jnp.float32) ** level_of(seeds[8], (LEV,), ((0, 4),), -0.2, 0.2)), 0.01, 0.1),
    }


def rotation_table():
    position = jnp.arange(64, dtype=jnp.int32)
    grid_row = position // 8
    grid_col = position % 8
    return jnp.stack([grid_row * 8 + grid_col, grid_col * 8 + (7 - grid_row), (7 - grid_row) * 8 + (7 - grid_col), (7 - grid_col) * 8 + grid_row]).astype(jnp.int32)


def reference(obs_forcing, transport_weights, block_offsets, edge_source, edge_target, edge_rotation, edge_weight, mixing_rate, flux_profile):
    blocks = TILES * BLK_DEV
    feature = TR * LEV
    obs_every = STEPS // NOBS
    level_index = jnp.arange(LEV, dtype=jnp.int32)
    mixing = jnp.where((level_index < LEV - 1)[:, None], mixing_rate, jnp.float32(0.0))
    mixing_ext = jnp.concatenate([jnp.zeros((1, COLS), jnp.float32), mixing], 0)
    block_ids = jnp.arange(blocks, dtype=jnp.int32)
    nearby = ((block_ids[:, None] + block_offsets) % blocks).astype(jnp.int32)
    tile_ids = jnp.arange(TILES, dtype=jnp.int32)
    source_global = tile_ids[:, None, None] * BLK_DEV + edge_source
    source_flat = jnp.transpose(source_global, (1, 0, 2)).reshape(-1).astype(jnp.int32)
    live_slot = edge_target < BLK_DEV
    target_flat = jnp.where(live_slot, tile_ids[:, None, None] * BLK_DEV + edge_target, 0).reshape(-1).astype(jnp.int32)
    live_flat = live_slot.reshape(-1).astype(jnp.float32)
    permuted_index = rotation_table()[edge_rotation.reshape(-1)]
    scale_rows = edge_weight.reshape(-1, BLOCK) * live_flat[:, None]
    block_groups = blocks // BLK_DEV

    def transport(adjoint):
        rounded = adjoint.reshape(feature, blocks, BLOCK).astype(jnp.bfloat16)

        def one_group(group_index):
            first_block = group_index * BLK_DEV
            near_rows = lax.dynamic_slice_in_dim(nearby, first_block, BLK_DEV, 0)
            weight_rows = lax.dynamic_slice_in_dim(transport_weights, first_block, BLK_DEV, 0)
            weight_rows = weight_rows.reshape(BLK_DEV, BLOCK, K, BLOCK)
            picked = rounded[:, near_rows, :].astype(jnp.float32)
            return jnp.einsum('fbkc,bdkc->bfd', picked, weight_rows.astype(jnp.float32), precision=lax.Precision.HIGHEST)

        moved_rows = lax.map(one_group, jnp.arange(block_groups, dtype=jnp.int32))
        moved_rows = moved_rows.reshape(blocks, feature, BLOCK).transpose(1, 0, 2)
        sent_rows = rounded[:, source_flat, :].astype(jnp.float32)
        rotated = jnp.take_along_axis(sent_rows, permuted_index[None], axis=2)
        edge_term = rotated * scale_rows[None]
        moved_rows = moved_rows.at[:, target_flat, :].add(edge_term)
        return moved_rows.reshape(TR, LEV, COLS)

    adjoint = jnp.zeros((TR, LEV, COLS), jnp.float32)
    gradient = jnp.zeros((TR, COLS), jnp.float32)
    for step_index in reversed(range(STEPS)):
        if step_index % obs_every == obs_every - 1:
            adjoint = adjoint + obs_forcing[step_index // obs_every].astype(jnp.float32)
        padded = jnp.pad(adjoint, ((0, 0), (1, 1), (0, 0)))
        flux_term = mixing_ext[None] * (padded[:, 1:] - padded[:, :-1])
        adjoint = adjoint + flux_term[:, 1:] - flux_term[:, :-1]
        adjoint = transport(adjoint)
        gradient = gradient + jnp.einsum('tlc,l->tc', adjoint, flux_profile, precision=lax.Precision.HIGHEST)
    return adjoint, gradient
```

```python
import functools

import jax
import jax.numpy as jnp
from jax import lax
from jax.experimental import pallas as pl
from jax.experimental.pallas import tpu as pltpu
from jax.sharding import PartitionSpec as P

LEV = 72
BLOCK = 64
HB = 4
EB = 2
STEPS = 16
NOBS = 4
LANES = 128
GROUP = 4


def passed_along(array, axis, by):
    devices = lax.axis_size(axis)
    pairs = [(i, i + by) for i in range(devices) if 0 <= i + by < devices]
    return lax.ppermute(array, axis, pairs)


def extended_2(block, sides, width, periodic):
    for axis, dim in sides:
        count = lax.axis_size(axis)
        forward = [(i, i + 1) for i in range(count - 1)]
        if periodic:
            forward.append((count - 1, 0))
        backward = [(target, source) for source, target in forward]
        low = lax.ppermute(
            lax.slice_in_dim(block, block.shape[dim] - width, None, axis=dim), axis, forward
        )
        high = lax.ppermute(lax.slice_in_dim(block, 0, width, axis=dim), axis, backward)
        block = jnp.concatenate([low, block, high], axis=dim)
    return block


def rotation_table():
    position = jnp.arange(64, dtype=jnp.int32)
    grid_row = position // 8
    grid_col = position % 8
    return jnp.stack(
        [
            grid_row * 8 + grid_col,
            grid_col * 8 + (7 - grid_row),
            (7 - grid_row) * 8 + (7 - grid_col),
            (7 - grid_col) * 8 + grid_row,
        ]
    )


def stepwise_body(
    obs_forcing,
    transport_weights,
    block_offsets,
    edge_source,
    edge_target,
    edge_rotation,
    edge_weight,
    mixing_rate,
    flux_profile,
):
    levels_dev = mixing_rate.shape[0]
    columns_dev = mixing_rate.shape[1]
    blocks_dev = columns_dev // BLOCK
    tracers = obs_forcing.shape[1]
    feature = tracers * levels_dev
    obs_every = STEPS // NOBS
    own_tile = lax.axis_index("tile")
    level_index = lax.axis_index("sub") * levels_dev + jnp.arange(levels_dev, dtype=jnp.int32)
    mixing = jnp.where((level_index < LEV - 1)[:, None], mixing_rate, jnp.float32(0.0))
    rate_below = passed_along(mixing[-1:], "sub", 1)
    mixing_ext = jnp.concatenate([rate_below, mixing], 0)
    nearby = jnp.arange(blocks_dev, dtype=jnp.int32)[:, None] + HB + block_offsets
    sources = lax.dynamic_index_in_dim(edge_source, own_tile, 0, keepdims=False).reshape(-1)
    target_flat = edge_target.reshape(-1)
    placement_matrix = (
        target_flat[:, None] == jnp.arange(blocks_dev, dtype=jnp.int32)[None, :]
    ).astype(jnp.float32)
    permuted_index = rotation_table()[edge_rotation.reshape(-1)]
    rotation_onehot = (
        jnp.arange(BLOCK, dtype=jnp.int32)[None, :, None] == permuted_index[:, None, :]
    ).astype(jnp.bfloat16)
    scale_rows = edge_weight.reshape(-1, BLOCK)
    span = transport_weights.shape[2]

    def transport(adjoint):
        rounded = adjoint.reshape(feature, columns_dev).astype(jnp.bfloat16)
        widened = extended_2(rounded, (("tile", 1),), HB * BLOCK, True)
        widened = widened.reshape(feature, blocks_dev + 2 * HB, BLOCK)
        picked = widened[:, nearby, :].reshape(feature, blocks_dev, span)
        moved_rows = jnp.einsum(
            "fbj,bdj->fbd", picked, transport_weights, preferred_element_type=jnp.float32
        )
        local_rows = rounded.reshape(feature, blocks_dev, BLOCK)
        received = lax.all_to_all(
            local_rows[:, sources, :], "tile", split_axis=1, concat_axis=1, tiled=True
        )
        rotated = jnp.einsum(
            "fsc,scp->fsp", received, rotation_onehot, preferred_element_type=jnp.float32
        )
        edge_term = jnp.einsum(
            "fsp,sb->fbp",
            rotated * scale_rows[None],
            placement_matrix,
            precision=lax.Precision.HIGHEST,
        )
        return (moved_rows + edge_term).reshape(tracers, levels_dev, columns_dev)

    def advance(step_count, state_pair):
        adjoint, gradient = state_pair
        step_index = STEPS - 1 - step_count
        obs_flag = (step_index % obs_every == obs_every - 1).astype(jnp.float32)
        forcing_now = lax.dynamic_index_in_dim(
            obs_forcing, step_index // obs_every, 0, keepdims=False
        ).astype(jnp.float32)
        adjoint = adjoint + obs_flag * forcing_now
        extended = extended_2(adjoint, (("sub", 1),), 1, False)
        flux_term = mixing_ext[None] * (extended[:, 1:] - extended[:, :-1])
        adjoint = adjoint + flux_term[:, 1:] - flux_term[:, :-1]
        adjoint = transport(adjoint)
        gradient = gradient + jnp.einsum(
            "tlc,l->tc", adjoint, flux_profile, precision=lax.Precision.HIGHEST
        )
        return (adjoint, gradient)

    initial = (
        jnp.zeros((tracers, levels_dev, columns_dev), jnp.float32),
        jnp.zeros((tracers, columns_dev), jnp.float32),
    )
    adjoint, gradient = lax.fori_loop(0, STEPS, advance, initial)
    flux_grad = lax.psum_scatter(
        gradient.astype(jnp.bfloat16), "sub", scatter_dimension=1, tiled=True
    ).astype(jnp.float32)
    return (adjoint, flux_grad)


def swap(array, axis, distance):
    count = lax.axis_size(axis)
    return lax.ppermute(array, axis, [(i, i ^ distance) for i in range(count)])


def transport_kernel(
    sizes,
    place,
    offsets,
    own_weights,
    sent_weights,
    edges,
    rate,
    forcing,
    profile,
    adjoint_out,
    gradient_out,
    band,
    even,
    odd,
):
    tiles, groups, rows, own_lo, own_hi, window, slots, tile_cols, members, subs = sizes
    own_tile, own_member, own_sub = place[0], place[1], place[2]
    total_cols = tiles * tile_cols
    wrap = HB * BLOCK // LANES
    lane_low = lax.broadcasted_iota(jnp.int32, (BLOCK, LANES), 1) < BLOCK
    half_slots = slots // 2
    share_of = own_member * subs + own_sub

    def clear(g, _):
        band[g] = jnp.zeros(band.shape[1:], band.dtype)
        return 0

    lax.fori_loop(0, tiles * groups, clear, 0, unroll=2)

    def add_group(d, g, piece):
        for q in range(GROUP):
            col = pl.ds((q // 2) * LANES, LANES)
            keep = lane_low if q % 2 == 0 else jnp.logical_not(lane_low)
            for k in range(slots):
                w = offsets[(d * groups + g) * GROUP * slots + q * slots + k] + (q + HB)
                part = jnp.where(keep, piece(k, col), jnp.zeros((), jnp.bfloat16))
                band[d * groups + g, w, :, col] = band[d * groups + g, w, :, col] + part

    def build_own(g, _):
        add_group(0, g, lambda k, col: own_weights[g, pl.ds(k * BLOCK, BLOCK), col])
        return 0

    lax.fori_loop(0, groups, build_own, 0)

    def build_sent(i, _):
        d = i // groups + 1
        g = lax.rem(i, groups)
        apart = lax.bitwise_xor(g, share_of)
        other_core = lax.rem(apart, 2)
        chip = apart // 2

        def piece(k, col):
            return sent_weights[
                k // half_slots, other_core, chip, d - 1,
                pl.ds((k % half_slots) * BLOCK, BLOCK), col,
            ]

        add_group(d, g, piece)
        return 0

    lax.fori_loop(0, (tiles - 1) * groups, build_sent, 0)

    def mixed(v, d, col):
        flux = rate[d, :, col] * (pltpu.roll(v, rows - 1, 0) - v)
        return (v + flux - pltpu.roll(flux, 1, 0)).astype(jnp.bfloat16)

    def close_ring(dst):
        for j in range(wrap):
            dst[j] = dst[total_cols + j]
            dst[total_cols + wrap + j] = dst[wrap + j]

    def start(d, _):
        base = lax.bitwise_xor(d, own_tile) * tile_cols
        for c in range(tile_cols):
            col = pl.ds(c * LANES, LANES)
            even[base + wrap + c] = mixed(
                forcing[NOBS - 1, d, :, col].astype(jnp.float32), d, col
            )
        return 0

    lax.fori_loop(0, tiles, start, 0)
    close_ring(even)
    gradient_out[...] = jnp.zeros(gradient_out.shape, jnp.float32)

    def advance(src, dst, slot):
        def one_tile(d, _):
            base = lax.bitwise_xor(d, own_tile) * tile_cols
            for g in range(groups):
                near = jnp.concatenate(
                    [src[base + 2 * g + j] for j in range(window // 2)], axis=1
                )
                matrix = band[d * groups + g].reshape(window * BLOCK, GROUP * BLOCK)
                moved = jnp.dot(near, matrix, preferred_element_type=jnp.float32)
                for h in range(2):
                    v = moved[:, h * LANES : (h + 1) * LANES]
                    if g == 0 and h == 0:
                        rim = jnp.concatenate(
                            [src[wrap + i * tile_cols] for i in range(tiles)], axis=1
                        )
                        v = v + jnp.dot(rim, edges[d], preferred_element_type=jnp.float32)
                    c = 2 * g + h
                    col = pl.ds(c * LANES, LANES)
                    own = v[own_lo:own_hi]
                    weighted = own * profile[...]
                    total = weighted[0:8]
                    for r in range(8, own_hi - own_lo, 8):
                        total = total + weighted[r : r + 8]
                    gradient_out[d, :, col] = gradient_out[d, :, col] + total
                    if slot is not None:
                        adjoint_out[d, :, col] = own
                        v = v + forcing[slot, d, :, col].astype(jnp.float32)
                    dst[base + wrap + c] = mixed(v, d, col)
            return 0

        lax.fori_loop(0, tiles, one_tile, 0)
        close_ring(dst)

    def cycle(n, _):
        for i in range(STEPS // NOBS):
            src, dst = (even, odd) if i % 2 == 0 else (odd, even)
            last = i == STEPS // NOBS - 1
            advance(src, dst, jnp.maximum(NOBS - 2 - n, 0) if last else None)
        return 0

    lax.fori_loop(0, NOBS, cycle, 0)


def gathered_body(
    obs_forcing,
    transport_weights,
    block_offsets,
    edge_source,
    edge_target,
    edge_rotation,
    edge_weight,
    mixing_rate,
    flux_profile,
):
    members, tiles, subs = (lax.axis_size(a) for a in ("member", "tile", "sub"))
    levels_dev, columns_dev = mixing_rate.shape
    blocks_dev = columns_dev // BLOCK
    groups = blocks_dev // GROUP
    slots = block_offsets.shape[1]
    span = slots * BLOCK
    per_pair = edge_target.shape[2]
    tile_cols = columns_dev // LANES
    window = GROUP + 2 * HB
    own_lo = levels_dev // 8 * 8
    own_hi = -(-2 * levels_dev // 8) * 8
    rows = -(-3 * levels_dev // 8) * 8
    m, t, s = (lax.axis_index(a) for a in ("member", "tile", "sub"))

    turned = transport_weights.reshape(groups, GROUP, BLOCK, span)
    share = lax.dynamic_index_in_dim(turned, m * subs + s, 0, keepdims=False)
    share = share.transpose(2, 0, 1).reshape(span, GROUP * BLOCK)
    own_weights = turned.transpose(0, 3, 1, 2).reshape(groups, span, GROUP * BLOCK)

    level_index = s * levels_dev + jnp.arange(levels_dev, dtype=jnp.int32)
    mixing = jnp.where((level_index < LEV - 1)[:, None], mixing_rate, jnp.float32(0.0))
    small = jnp.concatenate(
        [
            block_offsets.reshape(-1).astype(jnp.bfloat16),
            edge_target.reshape(-1).astype(jnp.bfloat16),
            edge_rotation.reshape(-1).astype(jnp.bfloat16),
            edge_weight.reshape(-1).astype(jnp.bfloat16),
        ]
    )
    small = jnp.pad(small, (0, columns_dev - small.shape[0]))[None]
    steady = jnp.concatenate([mixing.astype(jnp.bfloat16), small], 0)

    def forcing_for(d):
        return lax.dynamic_index_in_dim(obs_forcing, t ^ d, 1, keepdims=False)

    first, rest, far = [], [], []
    for d in range(tiles):
        f = forcing_for(d)
        a = jnp.concatenate([steady, f[NOBS - 1]], 0)
        b = f[: NOBS - 1]
        if d:
            a = swap(a, "tile", d)
            far.append(swap(share, "tile", d))
            b = swap(b, "tile", d)
        first.append(a)
        rest.append(b)
    first = jnp.stack(first)
    rest = jnp.stack(rest, 1)
    far = jnp.stack(far)

    up = [(i, i + 1) for i in range(subs - 1)]
    down = [(i + 1, i) for i in range(subs - 1)]

    def banded(own, dim):
        low = lax.ppermute(own, "sub", up)
        high = lax.ppermute(own, "sub", down)
        shape = list(own.shape)
        shape[dim] = rows - 3 * levels_dev
        return jnp.concatenate([low, own, high, jnp.zeros(shape, own.dtype)], dim)

    pair = jnp.stack([first[:, :levels_dev], first[:, levels_dev + 1 :]])
    pair = banded(pair, 2)
    rate = pair[0].astype(jnp.float32)
    forcing = jnp.concatenate([banded(rest, 2), pair[1][None]], 0)

    half = span // 2
    a0, b0 = far[:, :half], far[:, half:]
    a1 = swap(a0, "sub", 2)
    b1 = swap(b0, "member", 1)
    aa = jnp.stack([a0, a1])
    bb = jnp.stack([b0, b1])
    aa = jnp.concatenate([aa, swap(aa, "member", 1)], 0)
    b2 = swap(bb, "sub", 2)
    bb = jnp.stack([b0, b2[0], b1, b2[1]])
    mine = jnp.stack([aa, bb])
    sent = jnp.stack([mine, swap(mine, "sub", 1)], 1)

    small = first[:, levels_dev].astype(jnp.float32)
    n_off = blocks_dev * slots
    n_edge = tiles * per_pair
    offsets = small[:, :n_off].astype(jnp.int32).reshape(-1)
    target = small[:, n_off : n_off + n_edge].astype(jnp.int32)
    rotation = small[:, n_off + n_edge : n_off + 2 * n_edge].astype(jnp.int32)
    weight = small[:, n_off + 2 * n_edge : n_off + 2 * n_edge + n_edge * BLOCK]
    weight = weight.reshape(tiles, n_edge, BLOCK)
    source = edge_source[:, t ^ jnp.arange(tiles)].transpose(1, 0, 2).reshape(tiles, n_edge)
    turn = rotation_table()[rotation]
    edges = (
        (source[:, :, None, None, None, None] == jnp.arange(EB)[:, None, None, None])
        & (turn[:, :, None, None, None, :] == jnp.arange(BLOCK)[:, None, None])
        & (target[:, :, None, None, None, None] == jnp.arange(EB)[:, None])
    )
    edges = jnp.where(edges, weight[:, :, None, None, None, :], 0.0)
    edges = edges.reshape(tiles, tiles, per_pair, EB * BLOCK, EB * BLOCK).sum(2)
    edges = edges.reshape(tiles, tiles * EB * BLOCK, EB * BLOCK).astype(jnp.bfloat16)

    place = jnp.stack([t, m, s]).astype(jnp.int32)
    profile = jnp.pad(
        flux_profile, (levels_dev - own_lo, own_hi - 2 * levels_dev)
    )
    profile = jnp.broadcast_to(profile[:, None], (own_hi - own_lo, LANES))

    sizes = (tiles, groups, rows, own_lo, own_hi, window, slots, tile_cols, members, subs)
    ring = (tiles * tile_cols + 2 * HB * BLOCK // LANES, rows, LANES)
    smem = pl.BlockSpec(memory_space=pltpu.SMEM)
    vmem = pl.BlockSpec(memory_space=pltpu.VMEM)
    adjoint, gradient = pl.pallas_call(
        functools.partial(transport_kernel, sizes),
        out_shape=(
            jax.ShapeDtypeStruct((tiles, own_hi - own_lo, columns_dev), jnp.float32),
            jax.ShapeDtypeStruct((tiles, 8, columns_dev), jnp.float32),
        ),
        in_specs=[smem, smem] + [vmem] * 6,
        out_specs=(vmem, vmem),
        scratch_shapes=[
            pltpu.VMEM((tiles * groups, window, BLOCK, GROUP * BLOCK), jnp.bfloat16),
            pltpu.VMEM(ring, jnp.bfloat16),
            pltpu.VMEM(ring, jnp.bfloat16),
        ],
        compiler_params=pltpu.CompilerParams(vmem_limit_bytes=60000 * 1024),
    )(place, offsets, own_weights, sent, edges, rate, forcing, profile)

    skip = levels_dev - own_lo
    adjoint = adjoint[:, skip : skip + levels_dev].astype(jnp.bfloat16)
    gradient = gradient.sum(1)[:, None].astype(jnp.bfloat16)
    back = jnp.concatenate([adjoint, gradient], 1)
    parts = [back[0]] + [swap(back[d], "tile", d) for d in range(1, tiles)]
    whole = jnp.stack(parts)[t ^ jnp.arange(tiles)]
    adjoint = whole[:, :levels_dev].astype(jnp.float32)
    partial_sum = whole[:, levels_dev].reshape(tiles, subs, columns_dev // subs)

    def for_sub(d):
        return lax.dynamic_index_in_dim(partial_sum, s ^ d, 1, keepdims=False)

    flux_grad = for_sub(0).astype(jnp.float32)
    for d in range(1, subs):
        flux_grad = flux_grad + swap(for_sub(d), "sub", d).astype(jnp.float32)
    return adjoint, flux_grad


def gathers(mesh):
    members, tiles, subs = (mesh.shape[a] for a in ("member", "tile", "sub"))
    return (members, tiles, subs) == (2, 4, 4)


def solution(mesh):
    fits = gathers(mesh)
    return jax.shard_map(
        gathered_body if fits else stepwise_body,
        mesh=mesh,
        in_specs=(
            P("member", None, "sub", "tile"),
            P("tile", None, None),
            P("tile", None),
            P(),
            P("tile", None, None),
            P("tile", None, None),
            P("tile", None, None, None),
            P("sub", "tile"),
            P("sub"),
        ),
        out_specs=(P("member", "sub", "tile"), P("member", ("tile", "sub"))),
        check_vma=False,
    )
```

```python
import functools

import jax
import jax.numpy as jnp
from jax import lax
from jax.experimental import pallas as pl
from jax.experimental.pallas import tpu as pltpu
from jax.sharding import PartitionSpec as P

LEV = 72
BLOCK = 64
HB = 4
EB = 2
STEPS = 16
NOBS = 4
LANES = 128
GROUP = 4


def passed_along(array, axis, by):
    devices = lax.axis_size(axis)
    pairs = [(i, i + by) for i in range(devices) if 0 <= i + by < devices]
    return lax.ppermute(array, axis, pairs)


def extended_2(block, sides, width, periodic):
    for axis, dim in sides:
        count = lax.axis_size(axis)
        forward = [(i, i + 1) for i in range(count - 1)]
        if periodic:
            forward.append((count - 1, 0))
        backward = [(target, source) for source, target in forward]
        low = lax.ppermute(
            lax.slice_in_dim(block, block.shape[dim] - width, None, axis=dim), axis, forward
        )
        high = lax.ppermute(lax.slice_in_dim(block, 0, width, axis=dim), axis, backward)
        block = jnp.concatenate([low, block, high], axis=dim)
    return block


def rotation_table():
    position = jnp.arange(64, dtype=jnp.int32)
    grid_row = position // 8
    grid_col = position % 8
    return jnp.stack(
        [
            grid_row * 8 + grid_col,
            grid_col * 8 + (7 - grid_row),
            (7 - grid_row) * 8 + (7 - grid_col),
            (7 - grid_col) * 8 + grid_row,
        ]
    )


def stepwise_body(
    obs_forcing,
    transport_weights,
    block_offsets,
    edge_source,
    edge_target,
    edge_rotation,
    edge_weight,
    mixing_rate,
    flux_profile,
):
    levels_dev = mixing_rate.shape[0]
    columns_dev = mixing_rate.shape[1]
    blocks_dev = columns_dev // BLOCK
    tracers = obs_forcing.shape[1]
    feature = tracers * levels_dev
    obs_every = STEPS // NOBS
    own_tile = lax.axis_index("tile")
    level_index = lax.axis_index("sub") * levels_dev + jnp.arange(levels_dev, dtype=jnp.int32)
    mixing = jnp.where((level_index < LEV - 1)[:, None], mixing_rate, jnp.float32(0.0))
    rate_below = passed_along(mixing[-1:], "sub", 1)
    mixing_ext = jnp.concatenate([rate_below, mixing], 0)
    nearby = jnp.arange(blocks_dev, dtype=jnp.int32)[:, None] + HB + block_offsets
    sources = lax.dynamic_index_in_dim(edge_source, own_tile, 0, keepdims=False).reshape(-1)
    target_flat = edge_target.reshape(-1)
    placement_matrix = (
        target_flat[:, None] == jnp.arange(blocks_dev, dtype=jnp.int32)[None, :]
    ).astype(jnp.float32)
    permuted_index = rotation_table()[edge_rotation.reshape(-1)]
    rotation_onehot = (
        jnp.arange(BLOCK, dtype=jnp.int32)[None, :, None] == permuted_index[:, None, :]
    ).astype(jnp.bfloat16)
    scale_rows = edge_weight.reshape(-1, BLOCK)
    span = transport_weights.shape[2]

    def transport(adjoint):
        rounded = adjoint.reshape(feature, columns_dev).astype(jnp.bfloat16)
        widened = extended_2(rounded, (("tile", 1),), HB * BLOCK, True)
        widened = widened.reshape(feature, blocks_dev + 2 * HB, BLOCK)
        picked = widened[:, nearby, :].reshape(feature, blocks_dev, span)
        moved_rows = jnp.einsum(
            "fbj,bdj->fbd", picked, transport_weights, preferred_element_type=jnp.float32
        )
        local_rows = rounded.reshape(feature, blocks_dev, BLOCK)
        received = lax.all_to_all(
            local_rows[:, sources, :], "tile", split_axis=1, concat_axis=1, tiled=True
        )
        rotated = jnp.einsum(
            "fsc,scp->fsp", received, rotation_onehot, preferred_element_type=jnp.float32
        )
        edge_term = jnp.einsum(
            "fsp,sb->fbp",
            rotated * scale_rows[None],
            placement_matrix,
            precision=lax.Precision.HIGHEST,
        )
        return (moved_rows + edge_term).reshape(tracers, levels_dev, columns_dev)

    def advance(step_count, state_pair):
        adjoint, gradient = state_pair
        step_index = STEPS - 1 - step_count
        obs_flag = (step_index % obs_every == obs_every - 1).astype(jnp.float32)
        forcing_now = lax.dynamic_index_in_dim(
            obs_forcing, step_index // obs_every, 0, keepdims=False
        ).astype(jnp.float32)
        adjoint = adjoint + obs_flag * forcing_now
        extended = extended_2(adjoint, (("sub", 1),), 1, False)
        flux_term = mixing_ext[None] * (extended[:, 1:] - extended[:, :-1])
        adjoint = adjoint + flux_term[:, 1:] - flux_term[:, :-1]
        adjoint = transport(adjoint)
        gradient = gradient + jnp.einsum(
            "tlc,l->tc", adjoint, flux_profile, precision=lax.Precision.HIGHEST
        )
        return (adjoint, gradient)

    initial = (
        jnp.zeros((tracers, levels_dev, columns_dev), jnp.float32),
        jnp.zeros((tracers, columns_dev), jnp.float32),
    )
    adjoint, gradient = lax.fori_loop(0, STEPS, advance, initial)
    flux_grad = lax.psum_scatter(
        gradient.astype(jnp.bfloat16), "sub", scatter_dimension=1, tiled=True
    ).astype(jnp.float32)
    return (adjoint, flux_grad)


def swap(array, axis, distance):
    count = lax.axis_size(axis)
    return lax.ppermute(array, axis, [(i, i ^ distance) for i in range(count)])


def halo_depths():
    every = STEPS // NOBS
    return (STEPS, STEPS), tuple(every * (n + 1) for n in range(NOBS - 1))


SMEM = pl.BlockSpec(memory_space=pltpu.SMEM)
VMEM = pl.BlockSpec(memory_space=pltpu.VMEM)
HBM = pl.BlockSpec(memory_space=pl.ANY)


def cross(array, member_distance, sub_distance):
    members, subs = lax.axis_size("member"), lax.axis_size("sub")
    pairs = [
        (i * subs + j, (i ^ member_distance) * subs + (j ^ sub_distance))
        for i in range(members)
        for j in range(subs)
    ]
    return lax.ppermute(array, ("member", "sub"), pairs)


def pack_kernel(sizes, place, forcing, mixing, small, *messages):
    tiles, levels, columns = sizes
    first, later = messages[:tiles], messages[tiles:]
    first_space = first[0].shape[0] - 2 * levels - 1
    later_space = later[0].shape[0] - (NOBS - 1) * levels

    def zeros(count):
        return [jnp.zeros((count, LANES), jnp.float32)] if count else []

    for d in range(tiles):
        tracer = lax.bitwise_xor(place[0], d)

        def one(c, _):
            col = pl.ds(pl.multiple_of(c * LANES, LANES), LANES)

            def plane(slot):
                return forcing[slot, tracer, :, col].astype(jnp.float32)

            lines = [mixing[:, col], plane(NOBS - 1), small[:, col]] + zeros(first_space)
            first[d][:, col] = jnp.concatenate(lines, 0).astype(jnp.bfloat16)
            lines = [plane(n) for n in range(NOBS - 1)] + zeros(later_space)
            later[d][:, col] = jnp.concatenate(lines, 0).astype(jnp.bfloat16)
            return 0

        lax.fori_loop(0, columns // LANES, one, 0, unroll=4)


def halo_kernel(levels, depths, *refs):
    parts, (whole, upward, downward) = refs[:-3], refs[-3:]
    space = upward.shape[1] - sum(depths)
    fill = [jnp.zeros((space, LANES), jnp.float32)] if space else []
    for d, part in enumerate(parts):

        def one(c, _):
            col = pl.ds(pl.multiple_of(c * LANES, LANES), LANES)
            whole[d, :, col] = part[:, col]
            lines = part[:, col].astype(jnp.float32)
            top = [lines[(i + 1) * levels - n : (i + 1) * levels] for i, n in enumerate(depths)]
            bottom = [lines[i * levels : i * levels + n] for i, n in enumerate(depths)]
            upward[d, :, col] = jnp.concatenate(top + fill, 0).astype(jnp.bfloat16)
            downward[d, :, col] = jnp.concatenate(bottom + fill, 0).astype(jnp.bfloat16)
            return 0

        lax.fori_loop(0, whole.shape[2] // LANES, one, 0, unroll=4)


def halo_parts(levels, depths, parts):
    count, (lines, columns) = len(parts), parts[0].shape
    strip = (count, -(-sum(depths) // 8) * 8, columns)
    return pl.pallas_call(
        functools.partial(halo_kernel, levels, depths),
        out_shape=tuple(
            jax.ShapeDtypeStruct(shape, jnp.bfloat16)
            for shape in ((count, lines, columns), strip, strip)
        ),
        in_specs=[VMEM] * count,
        out_specs=(VMEM,) * 3,
        compiler_params=pltpu.CompilerParams(vmem_limit_bytes=20000 * 1024),
    )(*parts)


def clear(bands, lo, hi):
    def one(g, _):
        for band in bands:
            band[g] = jnp.zeros(band.shape[1:], band.dtype)
        return 0

    lax.fori_loop(lo, hi, one, 0, unroll=2)


def add_group(bands, spot, offsets, g, slots, weights):
    lane_low = lax.broadcasted_iota(jnp.int32, (BLOCK, LANES), 1) < BLOCK
    for k in range(slots):
        for side in range(2):
            keep = lane_low if side == 0 else jnp.logical_not(lane_low)
            for j, band in enumerate(bands):
                at = side + 2 * j
                w = offsets[(g * GROUP + at) * slots + k] + (at + HB)
                part = weights(k * BLOCK, j * LANES)
                part = jnp.where(keep, part, jnp.zeros((), jnp.bfloat16))
                band[spot, w] = band[spot, w] + part


def build_own_kernel(slots, offsets, weights, *bands):
    clear(bands, 0, bands[0].shape[0])

    def one(g, _):
        rows = weights[pl.ds(pl.multiple_of(g * GROUP, GROUP), GROUP)]
        turned = rows.reshape(GROUP * BLOCK, slots * BLOCK).T
        add_group(
            bands, g, offsets, g, slots,
            lambda row, col: turned[row : row + BLOCK, col : col + LANES],
        )
        return 0

    lax.fori_loop(0, bands[0].shape[0], one, 0)


def band_shape(groups):
    return (groups, GROUP + 2 * HB, BLOCK, LANES)


def build_own(offsets, slots, weights):
    shape = jax.ShapeDtypeStruct(band_shape(weights.shape[0] // GROUP), jnp.bfloat16)
    return pl.pallas_call(
        functools.partial(build_own_kernel, slots),
        out_shape=(shape,) * (GROUP * BLOCK // LANES),
        in_specs=[SMEM, VMEM],
        out_specs=(VMEM,) * (GROUP * BLOCK // LANES),
        compiler_params=pltpu.CompilerParams(vmem_limit_bytes=20000 * 1024),
    )(offsets, weights)


def transport_kernel(sizes, place, offsets, source, target, rotation, profile, *rest):
    tiles, groups, rows, levels, own_lo, own_hi, window, tile_cols, per_pair, slots = sizes
    first_depths, later_depths = halo_depths()
    halves = GROUP * BLOCK // LANES
    first, later, rest = rest[:3], rest[3:6], rest[6:]
    own_bands, sent, rest = rest[:halves], rest[halves : halves + groups], rest[halves + groups :]
    message, bands, rest = rest[0], rest[1 : 1 + halves], rest[1 + halves :]
    held, even, odd, final, gradient, rate, edges, own_sems, sent_sems = rest
    own_tile = place[0]
    total_cols = tiles * tile_cols
    wrap = HB * BLOCK // LANES

    own_copies = [
        pltpu.make_async_copy(own_bands[j], bands[j].at[pl.ds(0, groups)], own_sems.at[j])
        for j in range(halves)
    ]
    sent_copies = [
        pltpu.make_async_copy(sent[i], held.at[i], sent_sems.at[i]) for i in range(groups)
    ]
    for copy in sent_copies + own_copies:
        copy.start()
    clear(bands, groups, tiles * groups)

    def field(refs, plane, depths, d, col):
        low, own, high = (ref[d, :, col].astype(jnp.float32) for ref in refs)
        depth, at = depths[plane], sum(depths[:plane])
        edge = jnp.zeros((levels - depth, LANES), jnp.float32)
        lines = [edge, low[at : at + depth], own[plane * levels : (plane + 1) * levels]]
        lines += [high[at : at + depth], jnp.zeros((rows - 2 * levels - depth, LANES), jnp.float32)]
        return jnp.concatenate([x for x in lines if x.shape[0]], 0)

    def mixed(v, d, col):
        flux = rate[d, :, col] * (pltpu.roll(v, rows - 1, 0) - v)
        return (v + flux - pltpu.roll(flux, 1, 0)).astype(jnp.bfloat16)

    def close_ring(dst):
        for j in range(wrap):
            dst[j] = dst[total_cols + j]
            dst[total_cols + wrap + j] = dst[wrap + j]

    column = lax.broadcasted_iota(jnp.int32, (BLOCK, LANES), 0)
    lane = lax.broadcasted_iota(jnp.int32, (BLOCK, LANES), 1)
    spot = lax.rem(lane, BLOCK)
    side = 8
    down, over = spot // side, lax.rem(spot, side)
    turns = [
        side * down + over,
        side * over + (side - 1) - down,
        side * (side - 1 - down) + (side - 1) - over,
        side * (side - 1 - over) + down,
    ]
    half = lane // BLOCK

    def start(d, _):
        base = lax.bitwise_xor(d, own_tile) * tile_cols
        for c in range(tile_cols):
            col = pl.ds(c * LANES, LANES)
            rate[d, :, col] = field(first, 0, first_depths, d, col)
            even[base + wrap + c] = mixed(field(first, 1, first_depths, d, col), d, col)
        for i in range(tiles):
            for e in range(EB):
                total = jnp.zeros((BLOCK, LANES), jnp.float32)
                for n in range(per_pair):
                    at = i * per_pair + n
                    r = rotation[d, at]
                    pick = jnp.where(r == 0, turns[0], turns[1])
                    pick = jnp.where(r == 2, turns[2], pick)
                    pick = jnp.where(r == 3, turns[3], pick)
                    goes = jnp.where(source[d, at] == e, target[d, at], EB)
                    weight = first[1][d, :, pl.ds((2 + at) * LANES, LANES)]
                    weight = weight.astype(jnp.float32)[2 * levels : 2 * levels + 1]
                    hit = jnp.logical_and(pick == column, half == goes)
                    total = total + jnp.where(hit, weight, 0.0)
                edges[d, pl.ds((i * EB + e) * BLOCK, BLOCK), :] = total.astype(jnp.bfloat16)
        return 0

    lax.fori_loop(0, tiles, start, 0)
    for copy in sent_copies:
        copy.wait()

    def build(n, _):
        d = lax.div(n, groups)
        i = lax.rem(n, groups)
        g = lax.bitwise_xor(place[1], i)
        add_group(
            bands, (d + 1) * groups + g, offsets, (d + 1) * groups + g, slots,
            lambda row, col: held[i, d, pl.ds(row, BLOCK), pl.ds(col, LANES)],
        )
        return 0

    lax.fori_loop(0, (tiles - 1) * groups, build, 0, unroll=2)
    for copy in own_copies:
        copy.wait()
    close_ring(even)
    gradient[...] = jnp.zeros(gradient.shape, jnp.float32)

    def advance(src, dst, slot):
        def one_tile(d, _):
            base = lax.bitwise_xor(d, own_tile) * tile_cols
            for g in range(groups):
                near = jnp.concatenate(
                    [src[base + 2 * g + j] for j in range(window // 2)], axis=1
                )
                matrix = jnp.concatenate(
                    [b[d * groups + g].reshape(window * BLOCK, LANES) for b in bands], axis=1
                )
                moved = jnp.dot(near, matrix, preferred_element_type=jnp.float32)
                for h in range(2):
                    v = moved[:, h * LANES : (h + 1) * LANES]
                    if g == 0 and h == 0:
                        rim = jnp.concatenate(
                            [src[wrap + i * tile_cols] for i in range(tiles)], axis=1
                        )
                        v = v + jnp.dot(rim, edges[d], preferred_element_type=jnp.float32)
                    c = 2 * g + h
                    col = pl.ds(c * LANES, LANES)
                    own = v[own_lo:own_hi]
                    weighted = own * profile[...]
                    total = weighted[0:8]
                    for r in range(8, own_hi - own_lo, 8):
                        total = total + weighted[r : r + 8]
                    gradient[d, :, col] = gradient[d, :, col] + total
                    if slot is not None:
                        final[d, :, col] = own
                        v = v + slot(d, col)
                    dst[base + wrap + c] = mixed(v, d, col)
            return 0

        lax.fori_loop(0, tiles, one_tile, 0)
        close_ring(dst)

    def cycle(n, _):
        def next_forcing(d, col):
            value = field(later, NOBS - 2, later_depths, d, col)
            for slot in range(NOBS - 3, -1, -1):
                value = jnp.where(n == NOBS - 2 - slot, field(later, slot, later_depths, d, col), value)
            return value

        for i in range(STEPS // NOBS):
            src, dst = (even, odd) if i % 2 == 0 else (odd, even)
            last = i == STEPS // NOBS - 1
            advance(src, dst, next_forcing if last else None)
        return 0

    lax.fori_loop(0, NOBS, cycle, 0)

    skip = levels - own_lo
    space = message.shape[1] - levels - 1

    def pack(d, _):
        for c in range(tile_cols):
            col = pl.ds(c * LANES, LANES)
            lines = jnp.concatenate(
                [
                    final[d, skip : skip + levels, col],
                    gradient[d, :, col].sum(0, keepdims=True),
                    jnp.zeros((space, LANES), jnp.float32),
                ],
                0,
            )
            message[d, :, col] = lines.astype(jnp.bfloat16)
        return 0

    lax.fori_loop(0, tiles, pack, 0)


def gathered_body(
    obs_forcing,
    transport_weights,
    block_offsets,
    edge_source,
    edge_target,
    edge_rotation,
    edge_weight,
    mixing_rate,
    flux_profile,
):
    tiles, subs = (lax.axis_size(a) for a in ("tile", "sub"))
    levels_dev, columns_dev = mixing_rate.shape
    blocks_dev = columns_dev // BLOCK
    groups = blocks_dev // GROUP
    slots = block_offsets.shape[1]
    span = slots * BLOCK
    width = GROUP * BLOCK
    per_pair = edge_target.shape[2]
    tile_cols = columns_dev // LANES
    window = GROUP + 2 * HB
    own_lo = levels_dev // 8 * 8
    own_hi = -(-2 * levels_dev // 8) * 8
    rows = -(-3 * levels_dev // 8) * 8
    m, t, s = (lax.axis_index(a) for a in ("member", "tile", "sub"))
    place = jnp.stack([t, m * subs + s]).astype(jnp.int32)

    turned = transport_weights.reshape(groups, GROUP, BLOCK, span)
    share = lax.dynamic_index_in_dim(turned, m * subs + s, 0, keepdims=False)
    share = share.transpose(2, 0, 1).reshape(span, width)
    arrived = [swap(share, "tile", d) for d in range(1, tiles)]

    n_off = blocks_dev * slots
    n_edge = tiles * per_pair
    weight = edge_weight.reshape(n_edge, BLOCK)
    small = jnp.concatenate(
        [
            block_offsets.reshape(-1).astype(jnp.float32),
            edge_target.reshape(-1).astype(jnp.float32),
            edge_rotation.reshape(-1).astype(jnp.float32),
        ]
    )
    small = jnp.pad(small, (0, 2 * LANES - small.shape[0]))
    small = jnp.concatenate([small, jnp.concatenate([weight, weight], 1).reshape(-1)])
    small = jnp.pad(small, (0, columns_dev - small.shape[0]))[None]
    level_index = s * levels_dev + jnp.arange(levels_dev, dtype=jnp.int32)
    mixing = jnp.where((level_index < LEV - 1)[:, None], mixing_rate, jnp.float32(0.0))

    def lines(count):
        return jax.ShapeDtypeStruct((-(-count // 8) * 8, columns_dev), jnp.bfloat16)

    messages = pl.pallas_call(
        functools.partial(pack_kernel, (tiles, levels_dev, columns_dev)),
        out_shape=(lines(2 * levels_dev + 1),) * tiles
        + (lines((NOBS - 1) * levels_dev),) * tiles,
        in_specs=[SMEM] + [VMEM] * 3,
        out_specs=(VMEM,) * (2 * tiles),
        compiler_params=pltpu.CompilerParams(vmem_limit_bytes=20000 * 1024),
    )(place, obs_forcing, mixing, small)
    first, later = list(messages[:tiles]), list(messages[tiles:])
    first, _ = lax.optimization_barrier((first, arrived[-1]))
    first = [first[0]] + [swap(first[d], "tile", d) for d in range(1, tiles)]

    here = jnp.stack(arrived)
    beside = swap(here, "sub", 2)
    across = swap(here, "member", 1)
    corner = cross(here, 1, 2)
    later, _ = lax.optimization_barrier((later, first))
    later = [later[0]] + [swap(later[d], "tile", d) for d in range(1, tiles)]

    def banded(own, depths):
        own, upward, downward = halo_parts(levels_dev, depths, own)
        low = lax.ppermute(upward, "sub", [(i, i + 1) for i in range(subs - 1)])
        high = lax.ppermute(downward, "sub", [(i + 1, i) for i in range(subs - 1)])
        return low, own, high

    first_depths, later_depths = halo_depths()
    small = jnp.stack([f[2 * levels_dev, : 2 * LANES] for f in first]).astype(jnp.int32)
    first = banded(first, first_depths)
    later = banded(later, later_depths)

    offsets = small[:, :n_off]
    target = small[:, n_off : n_off + n_edge]
    rotation = small[:, n_off + n_edge : n_off + 2 * n_edge]
    source = edge_source[:, t ^ jnp.arange(tiles)].transpose(1, 0, 2).reshape(tiles, n_edge)

    own_bands = build_own(block_offsets.reshape(-1), slots, transport_weights)
    sent = []
    for part in (here, beside, across, corner):
        sent += [part, swap(part, "sub", 1)]

    profile = jnp.pad(
        flux_profile, (levels_dev - own_lo, own_hi - 2 * levels_dev)
    )
    profile = jnp.broadcast_to(profile[:, None], (own_hi - own_lo, LANES))

    sizes = (
        tiles, groups, rows, levels_dev, own_lo, own_hi, window, tile_cols, per_pair, slots,
    )
    ring = (tiles * tile_cols + 2 * HB * BLOCK // LANES, rows, LANES)
    message = pl.pallas_call(
        functools.partial(transport_kernel, sizes),
        out_shape=jax.ShapeDtypeStruct(
            (tiles, -(-(levels_dev + 1) // 8) * 8, columns_dev), jnp.bfloat16
        ),
        in_specs=[SMEM] * 5 + [VMEM] * 7 + [HBM] * (len(own_bands) + len(sent)),
        out_specs=VMEM,
        scratch_shapes=[
            *[pltpu.VMEM(band_shape(tiles * groups), jnp.bfloat16) for _ in own_bands],
            pltpu.VMEM((groups, tiles - 1, span, width), jnp.bfloat16),
            pltpu.VMEM(ring, jnp.bfloat16),
            pltpu.VMEM(ring, jnp.bfloat16),
            pltpu.VMEM((tiles, own_hi - own_lo, columns_dev), jnp.float32),
            pltpu.VMEM((tiles, 8, columns_dev), jnp.float32),
            pltpu.VMEM((tiles, rows, columns_dev), jnp.float32),
            pltpu.VMEM((tiles, tiles * EB * BLOCK, EB * BLOCK), jnp.bfloat16),
            pltpu.SemaphoreType.DMA((len(own_bands),)),
            pltpu.SemaphoreType.DMA((len(sent),)),
        ],
        compiler_params=pltpu.CompilerParams(vmem_limit_bytes=44000 * 1024),
    )(
        place, offsets.reshape(-1), source, target, rotation, profile,
        *first, *later, *own_bands, *sent,
    )

    parts = [message[0]] + [swap(message[d], "tile", d) for d in range(1, tiles)]
    whole = jnp.stack(parts)[t ^ jnp.arange(tiles)]
    adjoint = whole[:, :levels_dev].astype(jnp.float32)
    partial_sum = whole[:, levels_dev].reshape(tiles, subs, columns_dev // subs)

    def for_sub(d):
        return lax.dynamic_index_in_dim(partial_sum, s ^ d, 1, keepdims=False)

    flux_grad = for_sub(0).astype(jnp.float32)
    for d in range(1, subs):
        flux_grad = flux_grad + swap(for_sub(d), "sub", d).astype(jnp.float32)
    return adjoint, flux_grad


def gathers(mesh):
    members, tiles, subs = (mesh.shape[a] for a in ("member", "tile", "sub"))
    return (members, tiles, subs) == (2, 4, 4)


def solution(mesh):
    fits = gathers(mesh)
    return jax.shard_map(
        gathered_body if fits else stepwise_body,
        mesh=mesh,
        in_specs=(
            P("member", None, "sub", "tile"),
            P("tile", None, None),
            P("tile", None),
            P(),
            P("tile", None, None),
            P("tile", None, None),
            P("tile", None, None, None),
            P("sub", "tile"),
            P("sub"),
        ),
        out_specs=(P("member", "sub", "tile"), P("member", ("tile", "sub"))),
        check_vma=False,
    )
```
